256 devices in a mesh: lon: 32 (over z, x_lo, core), lat: 8 (over y, x_hi).
Axes of the slice: x: 4 (x_hi: 2, x_lo: 2; x = x_hi * 2 + x_lo), y: 4, z: 8, core: 2. Of those that a mesh axis runs over, the one named last changes fastest.
Arguments:
- field: bfloat16 [2, 256, 768, 128], P(None, 'lat', 'lon'), may hold values from -6 to 6
- cotangent: bfloat16 [2, 256, 768, 128], P(None, 'lat', 'lon'), may hold values from -6 to 6
- first_weights: bfloat16 [3, 3, 128, 128], replicated, may hold values from -0.1875 to 0.1875
- second_weights: bfloat16 [3, 3, 128, 128], replicated, may hold values from -0.1875 to 0.1875
Outputs:
- output: bfloat16 [2, 256, 768, 128], P(None, 'lat', 'lon')
- field_grad: bfloat16 [2, 256, 768, 128], P(None, 'lat', 'lon')
- first_grad: float32 [3, 3, 128, 128], replicated
- second_grad: float32 [3, 3, 128, 128], replicated
The draws below stay inside these ranges and needn't reach their ends.
All inputs are finite; a program needn't handle non-finite values.
Results may differ from the reference program's by a relative error of at most 0.0032.
Values may be sent and summed in bfloat16 or wider, within the bound.
A program may use at most 64 MiB of HBM per device.

```python
import jax
import jax.numpy as jnp

CH = 128
BATCH = 2
NLAT = 256
NLON = 768


def block_levels(rng, shape, cuts, low, top_value):
    gain = 1.0
    for position, shards_of in cuts:
        draws = jax.random.uniform(jax.random.fold_in(jax.random.fold_in(rng, 6), position), (shards_of,), jnp.float32, low / len(cuts), top_value / len(cuts))
        gain = gain * jnp.repeat(jnp.exp(draws), shape[position] // shards_of).reshape((-1,) + (1,) * (len(shape) - 1 - position))
    return gain


def centred(key, extent, deviation, reach, shards=(), held_as=jnp.bfloat16):
    gain = block_levels(key, extent, shards, -0.22, 0.18) if shards else 1.0
    values = jax.random.normal(key, extent, jnp.float32) * deviation * gain
    return jnp.minimum(jnp.maximum(values, -reach), reach).astype(held_as)


def setup_inputs(seed: int = 0) -> dict:
    seeds = jax.random.split(jax.random.key(seed), 5)
    field = centred(seeds[0], (BATCH, NLAT, NLON, CH), 1.0, 6.0, ((1, 8), (2, 32)))
    cotangent = centred(seeds[1], (BATCH, NLAT, NLON, CH), 1.0, 6.0, ((1, 8), (2, 32)))
    first_weights = centred(seeds[2], (3, 3, CH, CH), (9 * CH) ** -0.5, 0.1875)
    second_weights = centred(seeds[3], (3, 3, CH, CH), (9 * CH) ** -0.5, 0.1875)
    return {"field": field, "cotangent": cotangent, "first_weights": first_weights, "second_weights": second_weights}


def pad_sphere(grid):
    shift_by = NLON // 2
    upper_row = jnp.roll(grid[:, :1], shift_by, axis=2)
    lower_row = jnp.roll(grid[:, -1:], shift_by, axis=2)
    tall = jnp.concatenate([upper_row, grid, lower_row], axis=1)
    return jnp.concatenate([tall[:, :, -1:], tall, tall[:, :, :1]], axis=2)

def correlate(padded, weights):
    batch = padded.shape[0]
    rows = padded.shape[1] - 2
    cols = padded.shape[2] - 2
    width = weights.shape[3]
    total = jnp.zeros((batch * rows * cols, width), jnp.float32)
    for row_tap in range(3):
        for col_tap in range(3):
            window = padded[:, row_tap:row_tap + rows, col_tap:col_tap + cols].reshape(-1, padded.shape[3])
            total = total + jnp.dot(window, weights[row_tap, col_tap], preferred_element_type=jnp.float32)
    return total.reshape(batch, rows, cols, width)

def spread(grad, weights):
    rows = grad.shape[1]
    cols = grad.shape[2]
    zeroed = jnp.pad(grad, ((0, 0), (2, 2), (2, 2), (0, 0)))
    total = jnp.zeros((grad.shape[0] * (rows + 2) * (cols + 2), weights.shape[2]), jnp.float32)
    for row_tap in range(3):
        for col_tap in range(3):
            window = zeroed[:, 2 - row_tap:4 - row_tap + rows, 2 - col_tap:4 - col_tap + cols].reshape(-1, grad.shape[3])
            total = total + jnp.dot(window, weights[row_tap, col_tap].T, preferred_element_type=jnp.float32)
    return total.reshape(grad.shape[0], rows + 2, cols + 2, weights.shape[2])

def weight_terms(padded, grad):
    rows = grad.shape[1]
    cols = grad.shape[2]
    flat_grad = grad.reshape(-1, grad.shape[3])
    taps = []
    for row_tap in range(3):
        for col_tap in range(3):
            window = padded[:, row_tap:row_tap + rows, col_tap:col_tap + cols].reshape(-1, padded.shape[3])
            taps.append(jnp.dot(window.T, flat_grad, preferred_element_type=jnp.float32))
    return jnp.stack(taps).reshape(3, 3, padded.shape[3], grad.shape[3])

def unpad(full):
    base = jnp.zeros((full.shape[0], full.shape[1] - 2, full.shape[2] - 2, full.shape[3]), jnp.float32)
    outcome, pullback = jax.vjp(pad_sphere, base)
    return pullback(full)[0]

def reference(field, cotangent, first_weights, second_weights):
    field_pad = pad_sphere(field)
    pre = correlate(field_pad, first_weights)
    hidden = jax.nn.silu(pre).astype(jnp.bfloat16)
    hidden_pad = pad_sphere(hidden)
    output = (field.astype(jnp.float32) + correlate(hidden_pad, second_weights)).astype(jnp.bfloat16)
    hidden_grad = unpad(spread(cotangent, second_weights))
    sigma = jax.nn.sigmoid(pre)
    pre_grad = (hidden_grad * sigma * (1.0 + pre * (1.0 - sigma))).astype(jnp.bfloat16)
    field_grad = (cotangent.astype(jnp.float32) + unpad(spread(pre_grad, first_weights))).astype(jnp.bfloat16)
    second_grad = weight_terms(hidden_pad, cotangent)
    first_grad = weight_terms(field_pad, pre_grad)
    return (output, field_grad, first_grad, second_grad)
```

```python
import jax
import jax.numpy as jnp
from jax import lax
from jax.experimental import pallas as pl
from jax.experimental.pallas import tpu as pltpu
from jax.sharding import PartitionSpec as P

HALF = 576
PIECE = 40


def padded_2(block, sides, width, periodic):
    for axis, dim in sides:
        count = lax.axis_size(axis)
        forward = [(i, i + 1) for i in range(count - 1)]
        if periodic:
            forward.append((count - 1, 0))
        backward = [(target, source) for source, target in forward]
        low = lax.ppermute(
            lax.slice_in_dim(block, block.shape[dim] - width, None, axis=dim), axis, forward
        )
        high = lax.ppermute(lax.slice_in_dim(block, 0, width, axis=dim), axis, backward)
        block = jnp.concatenate([low, block, high], axis=dim)
    return block


def from_behind(block, axis, distance):
    devices = range(lax.axis_size(axis))
    route = [((i - distance) % len(devices), i) for i in devices]
    return lax.ppermute(block, axis, route)


def pad_field(grid):
    lat_index = lax.axis_index("lat")
    last_band = lax.axis_size("lat") - 1
    opposite = lax.axis_size("lon") // 2
    padded = padded_2(grid, (("lon", 2), ("lat", 1)), 1, True)
    edges = jnp.concatenate([padded[:, 1:2], padded[:, -2:-1]], axis=1)
    partner = from_behind(edges, "lon", opposite)
    upper_row = jnp.where(lat_index == 0, partner[:, 0:1], padded[:, 0:1])
    lower_row = jnp.where(lat_index == last_band, partner[:, 1:2], padded[:, -1:])
    return jnp.concatenate([upper_row, padded[:, 1:-1], lower_row], axis=1)


def correlate(padded, weights):
    batch = padded.shape[0]
    rows = padded.shape[1] - 2
    cols = padded.shape[2] - 2
    width = weights.shape[3]
    total = jnp.zeros((batch * rows * cols, width), jnp.float32)
    for row_tap in range(3):
        for col_tap in range(3):
            window = padded[:, row_tap : row_tap + rows, col_tap : col_tap + cols].reshape(
                -1, padded.shape[3]
            )
            total = total + jnp.dot(
                window, weights[row_tap, col_tap], preferred_element_type=jnp.float32
            )
    return total.reshape(batch, rows, cols, width)


def spread(grad, weights):
    rows = grad.shape[1]
    cols = grad.shape[2]
    zeroed = jnp.pad(grad, ((0, 0), (2, 2), (2, 2), (0, 0)))
    total = jnp.zeros((grad.shape[0] * (rows + 2) * (cols + 2), weights.shape[2]), jnp.float32)
    for row_tap in range(3):
        for col_tap in range(3):
            window = zeroed[
                :, 2 - row_tap : 4 - row_tap + rows, 2 - col_tap : 4 - col_tap + cols
            ].reshape(-1, grad.shape[3])
            total = total + jnp.dot(
                window, weights[row_tap, col_tap].T, preferred_element_type=jnp.float32
            )
    return total.reshape(grad.shape[0], rows + 2, cols + 2, weights.shape[2])


def fold_back(full):
    lat_index = lax.axis_index("lat")
    last_band = lax.axis_size("lat") - 1
    opposite = lax.axis_size("lon") // 2
    sides = jnp.concatenate([full[:, :, :1], full[:, :, -1:]], axis=2)
    beside_all = padded_2(sides, (("lon", 2),), 1, True)
    inner = full[:, :, 1:-1]
    inner = jnp.concatenate(
        [
            inner[:, :, :1] + beside_all[:, :, 0:1],
            inner[:, :, 1:-1],
            inner[:, :, -1:] + beside_all[:, :, 3:4],
        ],
        axis=2,
    )
    caps = jnp.concatenate([inner[:, :1], inner[:, -1:]], axis=1)
    band = padded_2(caps.astype(jnp.bfloat16), (("lat", 1),), 1, False).astype(caps.dtype)
    across = from_behind(caps.astype(jnp.bfloat16), "lon", opposite).astype(caps.dtype)
    first_add = band[:, 0:1] + jnp.where(lat_index == 0, across[:, 0:1], 0.0)
    last_add = band[:, 3:4] + jnp.where(lat_index == last_band, across[:, 1:2], 0.0)
    return jnp.concatenate(
        [inner[:, 1:2] + first_add, inner[:, 2:-2], inner[:, -2:-1] + last_add], axis=1
    )


def weight_terms(padded, grad):
    rows = grad.shape[1]
    cols = grad.shape[2]
    flat_grad = grad.reshape(-1, grad.shape[3])
    taps = []
    for row_tap in range(3):
        for col_tap in range(3):
            window = padded[:, row_tap : row_tap + rows, col_tap : col_tap + cols].reshape(
                -1, padded.shape[3]
            )
            taps.append(
                lax.dot_general(
                    window, flat_grad, (((0,), (0,)), ((), ())), preferred_element_type=jnp.float32
                )
            )
    return jnp.stack(taps).reshape(3, 3, padded.shape[3], grad.shape[3])


def positions():
    lon = lax.axis_index("lon")
    lat = lax.axis_index("lat")
    core = lon % 2
    x_lo = (lon // 2) % 2
    depth = lon // 4
    return lon, lat, core, x_lo, depth


def offset_of(piece):
    return pl.multiple_of(((9 * piece) // 2) * 8, 8)


class Sum:
    def __init__(self, partial, final, half, pair, plane, column, gathered, sems):
        self.partial, self.final = partial, final
        self.half, self.pair, self.plane, self.column, self.gathered = half, pair, plane, column, gathered
        self.pair_sem, self.plane_sem, self.column_sem, self.gather_sem, self.share_sem = sems
        self.lon, self.lat, self.core, self.x_lo, self.depth = positions()
        self.member = self.x_lo * 8 + self.lat

    def plane_peer(self, step):
        peer = (self.member + step) % 16
        return peer, {"lon": self.depth * 4 + (peer // 8) * 2 + self.core, "lat": peer % 8}

    def column_peer(self, step):
        peer = (self.depth + step) % 8
        return peer, {"lon": peer * 4 + self.x_lo * 2 + self.core, "lat": self.lat}

    def partner(self):
        return {"lon": self.lon + 1 - 2 * self.core, "lat": self.lat}

    def remote(self, src, dst, send, recv, device):
        return pltpu.make_async_remote_copy(
            src_ref=src, dst_ref=dst, send_sem=send, recv_sem=recv,
            device_id=device, device_id_type=pl.DeviceIdType.MESH,
        )

    def pair_copy(self):
        other = pl.multiple_of((1 - self.core) * HALF, 8)
        return self.remote(
            self.partial.at[pl.ds(other, HALF)], self.pair, self.pair_sem.at[0], self.pair_sem.at[1], self.partner()
        )

    def plane_copy(self, step, receiving=False):
        peer, device = self.plane_peer(step)
        slot = peer if receiving else self.member
        return self.remote(
            self.half.at[pl.ds(offset_of(peer), PIECE)], self.plane.at[slot],
            self.plane_sem.at[0, peer], self.plane_sem.at[1, slot], device,
        )

    def column_copy(self, step, receiving=False):
        peer, device = self.column_peer(step)
        slot = peer if receiving else self.depth
        return self.remote(
            self.column.at[self.depth], self.column.at[slot],
            self.column_sem.at[0, peer], self.column_sem.at[1, slot], device,
        )

    def gather_copy(self, step, receiving=False):
        peer, device = self.plane_peer(step)
        slot = peer if receiving else self.member
        return self.remote(
            self.gathered.at[self.core, self.member], self.gathered.at[self.core, slot],
            self.gather_sem.at[0, peer], self.gather_sem.at[1, slot], device,
        )

    def share_copy(self, half):
        return self.remote(
            self.gathered.at[half], self.gathered.at[half], self.share_sem.at[0], self.share_sem.at[1], self.partner()
        )

    def each(self, count, act):
        def step(index, carry):
            act(index)
            return carry

        lax.fori_loop(1, count, step, 0)

    def start(self):
        self.pair_copy().start()

    def to_plane(self):
        self.pair_copy().wait_recv()
        own = pl.multiple_of(self.core * HALF, 8)
        self.half[...] = self.partial[pl.ds(own, HALF)] + self.pair[...]
        self.each(16, lambda step: self.plane_copy(step).start())
        self.plane[self.member] = self.half[pl.ds(offset_of(self.member), PIECE)]

    def to_column(self):
        self.each(16, lambda step: self.plane_copy(step, True).wait_recv())
        total = self.plane[0]
        for member in range(1, 16):
            total = total + self.plane[member]
        self.column[self.depth] = total
        self.each(8, lambda step: self.column_copy(step).start())

    def to_gather(self):
        self.each(8, lambda step: self.column_copy(step, True).wait_recv())
        total = self.column[0]
        for plane in range(1, 8):
            total = total + self.column[plane]
        self.gathered[self.core, self.member] = total.astype(jnp.bfloat16)
        self.each(16, lambda step: self.gather_copy(step).start())

    def to_share(self):
        self.each(16, lambda step: self.gather_copy(step, True).wait_recv())
        self.share_copy(self.core).start()

    def finish(self):
        self.share_copy(1 - self.core).wait_recv()
        for half in range(2):
            for piece in range(16):
                first = half * HALF + ((9 * piece) // 2) * 8
                self.final[pl.ds(first, PIECE)] = self.gathered[half, piece]
        self.pair_copy().wait_send()
        self.each(16, lambda step: self.plane_copy(step).wait_send())
        self.each(8, lambda step: self.column_copy(step).wait_send())
        self.each(16, lambda step: self.gather_copy(step).wait_send())
        self.share_copy(self.core).wait_send()


def sum_scratch():
    return [
        pltpu.VMEM((HALF, 128), jnp.float32),
        pltpu.VMEM((HALF, 128), jnp.float32),
        pltpu.VMEM((16, PIECE, 128), jnp.float32),
        pltpu.VMEM((8, PIECE, 128), jnp.float32),
        pltpu.VMEM((2, 16, PIECE, 128), jnp.bfloat16),
        pltpu.SemaphoreType.DMA((2,)),
        pltpu.SemaphoreType.DMA((2, 16)),
        pltpu.SemaphoreType.DMA((2, 8)),
        pltpu.SemaphoreType.DMA((2, 16)),
        pltpu.SemaphoreType.DMA((2,)),
    ]


def sum_kernel(first, second, first_sum, second_sum, *scratch):
    sums = [
        Sum(second, second_sum, *scratch[:5], scratch[5:10]),
        Sum(first, first_sum, *scratch[10:15], scratch[15:20]),
    ]
    barrier = pltpu.get_barrier_semaphore()

    def greet(device):
        pl.semaphore_signal(barrier, inc=1, device_id=device, device_id_type=pl.DeviceIdType.MESH)

    greet(sums[0].partner())
    sums[0].each(16, lambda step: greet(sums[0].plane_peer(step)[1]))
    sums[0].each(8, lambda step: greet(sums[0].column_peer(step)[1]))
    pl.semaphore_wait(barrier, 23)
    for one in sums:
        one.start()
    for one in sums:
        one.to_plane()
    for one in sums:
        one.to_column()
    for one in sums:
        one.to_gather()
    for one in sums:
        one.to_share()
    for one in sums:
        one.finish()


def sum_all(first, second):
    vmem = pl.BlockSpec(memory_space=pltpu.VMEM)
    shape = jax.ShapeDtypeStruct((2 * HALF, 128), jnp.bfloat16)
    sums = pl.pallas_call(
        sum_kernel,
        out_shape=(shape, shape),
        in_specs=[vmem, vmem],
        out_specs=(vmem, vmem),
        scratch_shapes=sum_scratch() + sum_scratch(),
        compiler_params=pltpu.CompilerParams(collective_id=0, has_side_effects=True),
    )(first.reshape(-1, 128), second.reshape(-1, 128))
    return tuple(one.astype(jnp.float32).reshape(3, 3, 128, 128) for one in sums)


def body(field, cotangent, first_weights, second_weights):
    field_pad = pad_field(field)
    pre = correlate(field_pad, first_weights)
    hidden = jax.nn.silu(pre).astype(jnp.bfloat16)
    hidden_pad = pad_field(hidden)
    output = (field.astype(jnp.float32) + correlate(hidden_pad, second_weights)).astype(
        jnp.bfloat16
    )
    hidden_grad = fold_back(spread(cotangent, second_weights))
    sigma = jax.nn.sigmoid(pre)
    pre_grad = (hidden_grad * sigma * (1.0 + pre * (1.0 - sigma))).astype(jnp.bfloat16)
    field_grad = (
        cotangent.astype(jnp.float32) + fold_back(spread(pre_grad, first_weights))
    ).astype(jnp.bfloat16)
    second_part = weight_terms(hidden_pad, cotangent)
    first_part = weight_terms(field_pad, pre_grad)
    first_grad, second_grad = sum_all(first_part, second_part)
    return (output, field_grad, first_grad, second_grad)


def solution(mesh):
    return jax.shard_map(
        body,
        mesh=mesh,
        in_specs=(P(None, "lat", "lon", None), P(None, "lat", "lon", None), P(), P()),
        out_specs=(P(None, "lat", "lon", None), P(None, "lat", "lon", None), P(), P()),
        check_vma=False,
    )
```

```python
import jax
import jax.numpy as jnp
from jax import lax
from jax.experimental import pallas as pl
from jax.experimental.pallas import tpu as pltpu
from jax.sharding import PartitionSpec as P

HALF = 576
PIECE = 40
WIDE = 384
PAIRS, COLS = 16, 24
F32, BF16 = jnp.float32, jnp.bfloat16
SIDES = [(v, h) for v in (-1, 0, 1) for h in (-1, 0, 1) if (v, h) != (0, 0)]


def positions():
    lon = lax.axis_index("lon")
    lat = lax.axis_index("lat")
    core = lon % 2
    x_lo = (lon // 2) % 2
    depth = lon // 4
    return lon, lat, core, x_lo, depth


def offset_of(piece):
    return pl.multiple_of(((9 * piece) // 2) * 8, 8)


class Sum:
    def __init__(self, partial, final, half, pair, plane, column, gathered, sems):
        self.partial, self.final = partial, final
        self.half, self.pair, self.plane, self.column, self.gathered = half, pair, plane, column, gathered
        self.pair_sem, self.plane_sem, self.column_sem, self.gather_sem, self.share_sem = sems
        self.lon, self.lat, self.core, self.x_lo, self.depth = positions()
        self.member = self.x_lo * 8 + self.lat

    def plane_peer(self, step):
        peer = (self.member + step) % 16
        return peer, {"lon": self.depth * 4 + (peer // 8) * 2 + self.core, "lat": peer % 8}

    def column_peer(self, step):
        peer = (self.depth + step) % 8
        return peer, {"lon": peer * 4 + self.x_lo * 2 + self.core, "lat": self.lat}

    def partner(self):
        return {"lon": self.lon + 1 - 2 * self.core, "lat": self.lat}

    def remote(self, src, dst, send, recv, device):
        return pltpu.make_async_remote_copy(
            src_ref=src, dst_ref=dst, send_sem=send, recv_sem=recv,
            device_id=device, device_id_type=pl.DeviceIdType.MESH,
        )

    def pair_copy(self):
        other = pl.multiple_of((1 - self.core) * HALF, 8)
        return self.remote(
            self.partial.at[pl.ds(other, HALF)], self.pair, self.pair_sem.at[0], self.pair_sem.at[1], self.partner()
        )

    def plane_copy(self, step, receiving=False):
        peer, device = self.plane_peer(step)
        slot = peer if receiving else self.member
        return self.remote(
            self.half.at[pl.ds(offset_of(peer), PIECE)], self.plane.at[slot],
            self.plane_sem.at[0, peer], self.plane_sem.at[1, slot], device,
        )

    def column_copy(self, step, receiving=False):
        peer, device = self.column_peer(step)
        slot = peer if receiving else self.depth
        return self.remote(
            self.column.at[self.depth], self.column.at[slot],
            self.column_sem.at[0, peer], self.column_sem.at[1, slot], device,
        )

    def gather_copy(self, step, receiving=False):
        peer, device = self.plane_peer(step)
        slot = peer if receiving else self.member
        return self.remote(
            self.gathered.at[self.core, self.member], self.gathered.at[self.core, slot],
            self.gather_sem.at[0, peer], self.gather_sem.at[1, slot], device,
        )

    def share_copy(self, half):
        return self.remote(
            self.gathered.at[half], self.gathered.at[half], self.share_sem.at[0], self.share_sem.at[1], self.partner()
        )

    def each(self, count, act):
        def step(index, carry):
            act(index)
            return carry

        lax.fori_loop(1, count, step, 0)

    def start(self):
        self.pair_copy().start()

    def to_plane(self):
        self.pair_copy().wait_recv()
        own = pl.multiple_of(self.core * HALF, 8)
        self.half[...] = self.partial[pl.ds(own, HALF)] + self.pair[...]
        self.each(16, lambda step: self.plane_copy(step).start())
        self.plane[self.member] = self.half[pl.ds(offset_of(self.member), PIECE)]

    def to_column(self):
        self.each(16, lambda step: self.plane_copy(step, True).wait_recv())
        total = self.plane[0]
        for member in range(1, 16):
            total = total + self.plane[member]
        self.column[self.depth] = total
        self.each(8, lambda step: self.column_copy(step).start())

    def to_gather(self):
        self.each(8, lambda step: self.column_copy(step, True).wait_recv())
        total = self.column[0]
        for plane in range(1, 8):
            total = total + self.column[plane]
        self.gathered[self.core, self.member] = total.astype(jnp.bfloat16)
        self.each(16, lambda step: self.gather_copy(step).start())

    def to_share(self):
        self.each(16, lambda step: self.gather_copy(step, True).wait_recv())
        self.share_copy(self.core).start()

    def finish(self):
        self.share_copy(1 - self.core).wait_recv()
        for half in range(2):
            for piece in range(16):
                first = half * HALF + ((9 * piece) // 2) * 8
                self.final[pl.ds(first, PIECE)] = self.gathered[half, piece]
        self.pair_copy().wait_send()
        self.each(16, lambda step: self.plane_copy(step).wait_send())
        self.each(8, lambda step: self.column_copy(step).wait_send())
        self.each(16, lambda step: self.gather_copy(step).wait_send())
        self.share_copy(self.core).wait_send()


def sum_scratch():
    return [
        pltpu.VMEM((HALF, 128), jnp.float32),
        pltpu.VMEM((HALF, 128), jnp.float32),
        pltpu.VMEM((16, PIECE, 128), jnp.float32),
        pltpu.VMEM((8, PIECE, 128), jnp.float32),
        pltpu.VMEM((2, 16, PIECE, 128), jnp.bfloat16),
        pltpu.SemaphoreType.DMA((2,)),
        pltpu.SemaphoreType.DMA((2, 16)),
        pltpu.SemaphoreType.DMA((2, 8)),
        pltpu.SemaphoreType.DMA((2, 16)),
        pltpu.SemaphoreType.DMA((2,)),
    ]


class Halo:
    def __init__(self, block, packed, rows, cols, corners, sems):
        self.block, self.packed, self.rows, self.cols, self.corners, self.sems = block, packed, rows, cols, corners, sems
        self.lon, self.lat = lax.axis_index("lon"), lax.axis_index("lat")

    def crosses(self, v):
        return self.lat == (0 if v < 0 else 7)

    def device(self, v, h):
        if v == 0:
            return {"lon": (self.lon + h + 32) % 32, "lat": self.lat}
        crosses = self.crosses(v)
        lon = (self.lon + h + 32 + jnp.where(crosses, 16, 0)) % 32
        return {"lon": lon, "lat": jnp.where(crosses, self.lat, self.lat + v)}

    def copy(self, v, h, receiving=False):
        first = 0 if v < 0 else PAIRS - 1
        side = 0 if h < 0 else 1
        if receiving:
            across, along = (0 if v < 0 else 1), side
            row, col = v + 1, h + 1
        else:
            crosses = self.crosses(v) if v else False
            across = jnp.where(crosses, 0 if v < 0 else 1, 1 if v < 0 else 0) if v else 0
            along = 1 - side
            row, col = (jnp.where(crosses, v + 1, 1 - v) if v else 1), 1 - h
        if h == 0:
            source, target = self.block.at[:, first], self.rows.at[across]
        elif v == 0:
            source, target = self.packed.at[side], self.cols.at[along]
        else:
            source, target = self.packed.at[side, :, first], self.corners.at[across, along]
        return pltpu.make_async_remote_copy(
            src_ref=source, dst_ref=target,
            send_sem=self.sems.at[0, v + 1, h + 1], recv_sem=self.sems.at[1, row, col],
            device_id=self.device(v, h), device_id_type=pl.DeviceIdType.MESH,
        )

    def pack(self):
        self.packed[0] = self.block[:, :, :, 0:2, :]
        self.packed[1] = self.block[:, :, :, COLS - 2 : COLS, :]

    def send(self):
        for v, h in SIDES:
            self.copy(v, h).start()

    def place(self, wide):
        wide[:, 2:34, 2:26, :] = self.block[...].reshape(2, 32, COLS, 128).astype(F32)
        for v, h in SIDES:
            self.copy(v, h, True).wait_recv()
        for side in range(2):
            wide[:, 2:34, pl.ds(26 * side, 2), :] = self.cols[side].reshape(2, 32, 2, 128).astype(F32)
        for across in range(2):
            crosses = self.crosses(-1 if across == 0 else 1)
            for row in range(2):
                target = 34 * across + jnp.where(crosses, 1 - row, row)
                wide[:, target, 2:26, :] = self.rows[across, :, row].astype(F32)
                for side in range(2):
                    wide[:, target, pl.ds(26 * side, 2), :] = self.corners[across, side, :, row].astype(F32)

    def close(self):
        for v, h in SIDES:
            self.copy(v, h).wait_send()


def halo_scratch():
    return [
        pltpu.VMEM((2, 2, PAIRS, 2, 2, 128), BF16),
        pltpu.VMEM((2, 2, 2, COLS, 128), BF16),
        pltpu.VMEM((2, 2, PAIRS, 2, 2, 128), BF16),
        pltpu.VMEM((2, 2, 2, 2, 2, 128), BF16),
        pltpu.SemaphoreType.DMA((2, 3, 3)),
    ]


def each_sample(act):
    def step(n, carry):
        act(n)
        return carry

    lax.fori_loop(0, 2, step, 0)


def lay_taps(wide, taps, rows):
    flat = wide.reshape(2, wide.shape[1] * 32, 128)

    def one(n):
        for b in range(3):
            shifted = flat[n, pl.ds(b, rows * 32), :].astype(BF16)
            taps[n, :, :, :, b * 128 : (b + 1) * 128] = shifted.reshape(rows // 2, 2, 32, 128)

    each_sample(one)


def pair_rows(taps, n, pairs):
    parts = [taps[n, q // 2 : q // 2 + pairs, q % 2].reshape(pairs * 32, WIDE) for q in range(4)]
    return jnp.concatenate(parts, axis=1)


def forward(taps, matrix, n, pairs):
    got = jnp.dot(pair_rows(taps, n, pairs), matrix[...], preferred_element_type=F32)
    return got.reshape(pairs, 32, 256)


def turned(left, right):
    return lax.dot_general(left, right, (((1,), (1,)), ((), ())), preferred_element_type=F32)


def backward(taps, matrix, n, pairs):
    return turned(pair_rows(taps, n, pairs), matrix[...]).reshape(pairs, 32, 256)


def lay_weights(weights, ahead, back):
    for q in range(4):
        for o in range(2):
            for b in range(3):
                tap, span = q - o, pl.ds(q * WIDE + b * 128, 128)
                inside = 0 <= tap <= 2
                lanes = pl.ds(o * 128, 128)
                ahead[span, lanes] = weights[tap * 3 + b] if inside else jnp.zeros((128, 128), BF16)
                back[lanes, span] = weights[(2 - tap) * 3 + 2 - b] if inside else jnp.zeros((128, 128), BF16)


def outer_sum(taps, grads, result, rows):
    total = None
    for n in range(2):
        part = lax.dot_general(
            taps[n].reshape(rows * 32, WIDE), grads[n].reshape(rows * 32, WIDE),
            (((0,), (0,)), ((), ())), preferred_element_type=F32,
        )
        total = part if total is None else total + part
    for a in range(3):
        for b in range(3):
            result[pl.ds((3 * a + b) * 128, 128)] = total[b * 128 : (b + 1) * 128, a * 128 : (a + 1) * 128]


def block_kernel(field, cotangent, w_one, w_two, output, field_grad, first_sum, second_sum, *scratch):
    (wide_f, wide_c, wide_h, wide_p, taps_f, taps_c, taps_h, taps_p, pre, grads_c, grads_p,
     ahead_one, back_one, ahead_two, back_two, first, second) = scratch[:17]
    halo_f = Halo(field, *scratch[17:22])
    halo_c = Halo(cotangent, *scratch[22:27])
    sum_two = Sum(second, second_sum, *scratch[27:32], scratch[32:37])
    sum_one = Sum(first, first_sum, *scratch[37:42], scratch[42:47])
    lat = lax.axis_index("lat")
    top = lat == 0
    at_pole = jnp.logical_or(top, lat == 7)

    barrier = pltpu.get_barrier_semaphore()

    def greet(device):
        pl.semaphore_signal(barrier, inc=1, device_id=device, device_id_type=pl.DeviceIdType.MESH)

    for v, h in SIDES:
        greet(halo_f.device(v, h))
    greet(sum_one.partner())
    sum_one.each(16, lambda step: greet(sum_one.plane_peer(step)[1]))
    sum_one.each(8, lambda step: greet(sum_one.column_peer(step)[1]))
    halo_f.pack()
    halo_c.pack()
    pl.semaphore_wait(barrier, 31)
    halo_f.send()
    halo_c.send()

    lay_weights(w_one, ahead_one, back_one)
    lay_weights(w_two, ahead_two, back_two)
    for wide in (wide_f, wide_c):
        wide[:, 0:36, 28:32, :] = jnp.zeros((2, 36, 4, 128), F32)
        wide[:, 36, :, :] = jnp.zeros((2, 32, 128), F32)
    for wide in (wide_h, wide_p):
        wide[:, 34, :, :] = jnp.zeros((2, 32, 128), F32)
    grads_c[...] = jnp.zeros(grads_c.shape, BF16)
    grads_p[...] = jnp.zeros(grads_p.shape, BF16)
    for a in range(3):
        grads_c[:, a : a + 32, 0:24, a * 128 : (a + 1) * 128] = cotangent[...].reshape(2, 32, COLS, 128)

    halo_f.place(wide_f)
    lay_taps(wide_f, taps_f, 36)

    def pre_one(n):
        got = forward(taps_f, ahead_one, n, 17)
        for o in range(2):
            pre[n, pl.ds(o, 17, stride=2)] = got[:, :, o * 128 : (o + 1) * 128]

    each_sample(pre_one)

    @pl.when(at_pole)
    def _():
        row = jnp.where(top, 0, 33)
        for n in range(2):
            got = None
            for q in range(3):
                right = w_one[pl.ds(3 * (2 - q), 3)].reshape(WIDE, 128)
                part = jnp.dot(taps_f[n, (row + q) // 2, (row + q) % 2], right, preferred_element_type=F32)
                got = part if got is None else got + part
            pre[n, row] = got

    def hidden_one(n):
        value = pre[n]
        wide_h[n, 0:34] = value / (1.0 + jnp.exp(-value))

    each_sample(hidden_one)
    lay_taps(wide_h, taps_h, 34)
    outer_sum(taps_h, grads_c, second, 34)
    sum_two.start()

    halo_c.place(wide_c)
    lay_taps(wide_c, taps_c, 36)

    def hidden_grad_one(n):
        got = backward(taps_c, back_two, n, 17)
        for o in range(2):
            wide_p[n, pl.ds(o, 17, stride=2)] = got[:, :, o * 128 : (o + 1) * 128]

    each_sample(hidden_grad_one)
    sign = jnp.where(top, 1.0, -1.0)

    @pl.when(at_pole)
    def _():
        row = jnp.where(top, 0, 32)
        source = jnp.where(top, 0, 17)
        for n in range(2):
            left = taps_c[n, source].reshape(64, WIDE)
            change = turned(left, back_two[0:128, 768:1152]) - turned(left, back_two[0:128, 0:384])
            wide_p[n, pl.ds(row, 2)] += (sign * change).reshape(2, 32, 128)

    def pre_grad_one(n):
        value = pre[n]
        s = 1.0 / (1.0 + jnp.exp(-value))
        grad = wide_p[n, 0:34] * s * (1.0 + value * (1.0 - s))
        wide_p[n, 0:34] = grad
        place = lax.broadcasted_iota(jnp.int32, (32, 32, 128), 1)
        inner = jnp.where(jnp.logical_and(place >= 1, place <= 24), grad[1:33], 0.0).astype(BF16)
        for a in range(3):
            grads_p[n, pl.ds(1 + a, 32), :, a * 128 : (a + 1) * 128] = inner

    each_sample(pre_grad_one)
    sum_two.to_plane()
    outer_sum(taps_f, grads_p, first, 36)
    sum_one.start()
    sum_two.to_column()

    def output_one(n):
        got = forward(taps_h, ahead_two, n, 16)
        for o in range(2):
            kept = got[:, 0:24, o * 128 : (o + 1) * 128]
            output[n, :, o] = (field[n, :, o].astype(F32) + kept).astype(BF16)

    each_sample(output_one)
    sum_one.to_plane()
    sum_two.to_gather()
    lay_taps(wide_p, taps_p, 34)

    def field_grad_one(n):
        got = backward(taps_p, back_one, n, 16)
        for o in range(2):
            wide_f[n, pl.ds(o, 16, stride=2)] = got[:, :, o * 128 : (o + 1) * 128]

    each_sample(field_grad_one)

    @pl.when(at_pole)
    def _():
        row = jnp.where(top, 0, 31)
        source = jnp.where(top, 0, 33)
        for n in range(2):
            left = taps_p[n, source // 2, source % 2]
            change = turned(left, back_one[0:128, 768:1152]) - turned(left, back_one[0:128, 0:384])
            wide_f[n, row] += sign * change

    sum_one.to_column()

    def keep_one(n):
        kept = wide_f[n, 0:32, 0:24].reshape(PAIRS, 2, COLS, 128)
        field_grad[n] = (cotangent[n].astype(F32) + kept).astype(BF16)

    each_sample(keep_one)
    sum_two.to_share()
    sum_one.to_gather()
    sum_two.finish()
    sum_one.to_share()
    sum_one.finish()
    halo_f.close()
    halo_c.close()


def body(field, cotangent, first_weights, second_weights):
    vmem = pl.BlockSpec(memory_space=pltpu.VMEM)
    grad = jax.ShapeDtypeStruct((2 * HALF, 128), BF16)
    cells = jax.ShapeDtypeStruct((2, PAIRS, 2, COLS, 128), BF16)
    matrix = [pltpu.VMEM((4 * WIDE, 256), BF16), pltpu.VMEM((256, 4 * WIDE), BF16)]
    output, field_grad, first, second = pl.pallas_call(
        block_kernel,
        out_shape=(cells, cells, grad, grad),
        in_specs=[vmem] * 4,
        out_specs=(vmem,) * 4,
        scratch_shapes=[
            pltpu.VMEM((2, 37, 32, 128), F32),
            pltpu.VMEM((2, 37, 32, 128), F32),
            pltpu.VMEM((2, 35, 32, 128), F32),
            pltpu.VMEM((2, 35, 32, 128), F32),
            pltpu.VMEM((2, 18, 2, 32, WIDE), BF16),
            pltpu.VMEM((2, 18, 2, 32, WIDE), BF16),
            pltpu.VMEM((2, 17, 2, 32, WIDE), BF16),
            pltpu.VMEM((2, 17, 2, 32, WIDE), BF16),
            pltpu.VMEM((2, 34, 32, 128), F32),
            pltpu.VMEM((2, 34, 32, WIDE), BF16),
            pltpu.VMEM((2, 36, 32, WIDE), BF16),
        ]
        + matrix
        + matrix
        + [pltpu.VMEM((2 * HALF, 128), F32)] * 2
        + halo_scratch()
        + halo_scratch()
        + sum_scratch()
        + sum_scratch(),
        compiler_params=pltpu.CompilerParams(
            collective_id=0, has_side_effects=True, vmem_limit_bytes=60 * 1024 * 1024
        ),
    )(field.reshape(cells.shape), cotangent.reshape(cells.shape), first_weights.reshape(9, 128, 128), second_weights.reshape(9, 128, 128))
    first, second = (one.astype(F32).reshape(3, 3, 128, 128) for one in (first, second))
    return output.reshape(field.shape), field_grad.reshape(field.shape), first, second


def solution(mesh):
    return jax.shard_map(
        body,
        mesh=mesh,
        in_specs=(P(None, "lat", "lon", None), P(None, "lat", "lon", None), P(), P()),
        out_specs=(P(None, "lat", "lon", None), P(None, "lat", "lon", None), P(), P()),
        check_vma=False,
    )
```

```python
import jax
import jax.numpy as jnp
from jax import lax
from jax.experimental import pallas as pl
from jax.experimental.pallas import tpu as pltpu
from jax.sharding import PartitionSpec as P

HALF = 576
PIECE = 40
WIDE = 384
PAIRS, COLS = 16, 24
F32, BF16 = jnp.float32, jnp.bfloat16
SIDES = [(v, h) for v in (-1, 0, 1) for h in (-1, 0, 1) if (v, h) != (0, 0)]


def positions():
    lon = lax.axis_index("lon")
    lat = lax.axis_index("lat")
    core = lon % 2
    x_lo = (lon // 2) % 2
    depth = lon // 4
    return lon, lat, core, x_lo, depth


class Sum:
    def __init__(self, partial, gathered, half, pair, plane, column, sems):
        self.partial, self.gathered = partial, gathered
        self.half, self.pair, self.plane, self.column = half, pair, plane, column
        self.pair_sem, self.plane_sem, self.column_sem, self.gather_sem, self.share_sem = sems
        self.lon, self.lat, self.core, self.x_lo, self.depth = positions()
        self.member = self.x_lo * 8 + self.lat

    def plane_peer(self, step):
        peer = (self.member + step) % 16
        return peer, {"lon": self.depth * 4 + (peer // 8) * 2 + self.core, "lat": peer % 8}

    def column_peer(self, step):
        peer = (self.depth + step) % 8
        return peer, {"lon": peer * 4 + self.x_lo * 2 + self.core, "lat": self.lat}

    def partner(self):
        return {"lon": self.lon + 1 - 2 * self.core, "lat": self.lat}

    def remote(self, src, dst, send, recv, device):
        return pltpu.make_async_remote_copy(
            src_ref=src, dst_ref=dst, send_sem=send, recv_sem=recv,
            device_id=device, device_id_type=pl.DeviceIdType.MESH,
        )

    def pair_copy(self):
        other = pl.multiple_of((1 - self.core) * HALF, 8)
        return self.remote(
            self.partial.at[pl.ds(other, HALF)], self.pair, self.pair_sem.at[0], self.pair_sem.at[1], self.partner()
        )

    def plane_copy(self, step, receiving=False):
        peer, device = self.plane_peer(step)
        slot = peer if receiving else self.member
        return self.remote(
            self.half.at[peer], self.plane.at[slot],
            self.plane_sem.at[0, peer], self.plane_sem.at[1, slot], device,
        )

    def column_copy(self, step, receiving=False):
        peer, device = self.column_peer(step)
        slot = peer if receiving else self.depth
        return self.remote(
            self.column.at[self.depth], self.column.at[slot],
            self.column_sem.at[0, peer], self.column_sem.at[1, slot], device,
        )

    def gather_copy(self, step, receiving=False):
        peer, device = self.plane_peer(step)
        slot = peer if receiving else self.member
        return self.remote(
            self.gathered.at[self.core, self.member], self.gathered.at[self.core, slot],
            self.gather_sem.at[0, peer], self.gather_sem.at[1, slot], device,
        )

    def share_copy(self, half):
        return self.remote(
            self.gathered.at[half], self.gathered.at[half], self.share_sem.at[0], self.share_sem.at[1], self.partner()
        )

    def each(self, count, act):
        def step(index, carry):
            act(index)
            return carry

        lax.fori_loop(1, count, step, 0)

    def start(self):
        self.pair_copy().start()

    def to_plane(self):
        self.pair_copy().wait_recv()
        own = pl.multiple_of(self.core * HALF, 8)
        for piece in range(16):
            first = ((9 * piece) // 2) * 8
            mine = self.partial[pl.ds(pl.multiple_of(own + first, 8), PIECE)]
            self.half[piece] = (mine + self.pair[pl.ds(first, PIECE)]).astype(BF16)
        self.each(16, lambda step: self.plane_copy(step).start())
        self.plane[self.member] = self.half[self.member]

    def to_column(self):
        self.each(16, lambda step: self.plane_copy(step, True).wait_recv())
        total = self.plane[0].astype(F32)
        for member in range(1, 16):
            total = total + self.plane[member].astype(F32)
        self.column[self.depth] = total
        self.each(8, lambda step: self.column_copy(step).start())

    def to_gather(self):
        self.each(8, lambda step: self.column_copy(step, True).wait_recv())
        total = self.column[0]
        for plane in range(1, 8):
            total = total + self.column[plane]
        self.gathered[self.core, self.member] = total.astype(jnp.bfloat16)
        self.each(16, lambda step: self.gather_copy(step).start())

    def to_share(self):
        self.each(16, lambda step: self.gather_copy(step, True).wait_recv())
        self.share_copy(self.core).start()

    def finish(self):
        self.share_copy(1 - self.core).wait_recv()
        self.pair_copy().wait_send()
        self.each(16, lambda step: self.plane_copy(step).wait_send())
        self.each(8, lambda step: self.column_copy(step).wait_send())
        self.each(16, lambda step: self.gather_copy(step).wait_send())
        self.share_copy(self.core).wait_send()


def sum_scratch():
    return [
        pltpu.VMEM((16, PIECE, 128), BF16),
        pltpu.VMEM((HALF, 128), F32),
        pltpu.VMEM((16, PIECE, 128), BF16),
        pltpu.VMEM((8, PIECE, 128), F32),
        pltpu.SemaphoreType.DMA((2,)),
        pltpu.SemaphoreType.DMA((2, 16)),
        pltpu.SemaphoreType.DMA((2, 8)),
        pltpu.SemaphoreType.DMA((2, 16)),
        pltpu.SemaphoreType.DMA((2,)),
    ]


class Halo:
    def __init__(self, block, packed, rows, cols, corners, sems):
        self.block, self.packed, self.rows, self.cols, self.corners, self.sems = block, packed, rows, cols, corners, sems
        self.lon, self.lat = lax.axis_index("lon"), lax.axis_index("lat")

    def crosses(self, v):
        return self.lat == (0 if v < 0 else 7)

    def device(self, v, h):
        if v == 0:
            return {"lon": (self.lon + h + 32) % 32, "lat": self.lat}
        crosses = self.crosses(v)
        lon = (self.lon + h + 32 + jnp.where(crosses, 16, 0)) % 32
        return {"lon": lon, "lat": jnp.where(crosses, self.lat, self.lat + v)}

    def copy(self, v, h, receiving=False):
        first = 0 if v < 0 else PAIRS - 1
        side = 0 if h < 0 else 1
        if receiving:
            across, along = (0 if v < 0 else 1), side
            row, col = v + 1, h + 1
        else:
            crosses = self.crosses(v) if v else False
            across = jnp.where(crosses, 0 if v < 0 else 1, 1 if v < 0 else 0) if v else 0
            along = 1 - side
            row, col = (jnp.where(crosses, v + 1, 1 - v) if v else 1), 1 - h
        if h == 0:
            source, target = self.block.at[:, first], self.rows.at[across]
        elif v == 0:
            source, target = self.packed.at[side], self.cols.at[along]
        else:
            source, target = self.packed.at[side, :, first], self.corners.at[across, along]
        return pltpu.make_async_remote_copy(
            src_ref=source, dst_ref=target,
            send_sem=self.sems.at[0, v + 1, h + 1], recv_sem=self.sems.at[1, row, col],
            device_id=self.device(v, h), device_id_type=pl.DeviceIdType.MESH,
        )

    def pack(self):
        self.packed[0] = self.block[:, :, :, 0:2, :]
        self.packed[1] = self.block[:, :, :, COLS - 2 : COLS, :]

    def send(self):
        for v, h in SIDES:
            self.copy(v, h).start()

    def fill(self, wide):
        wide[:, 2:34, 2:26, :] = self.block[...].reshape(2, 32, COLS, 128).astype(F32)
        wide[:, 0:36, 28:32, :] = jnp.zeros((2, 36, 4, 128), F32)
        wide[:, 36, :, :] = jnp.zeros((2, 32, 128), F32)

    def place(self, wide):
        for v, h in SIDES:
            self.copy(v, h, True).wait_recv()
        for side in range(2):
            wide[:, 2:34, pl.ds(26 * side, 2), :] = self.cols[side].reshape(2, 32, 2, 128).astype(F32)
        for across in range(2):
            crosses = self.crosses(-1 if across == 0 else 1)
            for row in range(2):
                target = 34 * across + jnp.where(crosses, 1 - row, row)
                wide[:, target, 2:26, :] = self.rows[across, :, row].astype(F32)
                for side in range(2):
                    wide[:, target, pl.ds(26 * side, 2), :] = self.corners[across, side, :, row].astype(F32)

    def close(self):
        for v, h in SIDES:
            self.copy(v, h).wait_send()


def halo_scratch():
    return [
        pltpu.VMEM((2, 2, PAIRS, 2, 2, 128), BF16),
        pltpu.VMEM((2, 2, 2, COLS, 128), BF16),
        pltpu.VMEM((2, 2, PAIRS, 2, 2, 128), BF16),
        pltpu.VMEM((2, 2, 2, 2, 2, 128), BF16),
        pltpu.SemaphoreType.DMA((2, 3, 3)),
    ]


def each_sample(act):
    def step(n, carry):
        act(n)
        return carry

    lax.fori_loop(0, 2, step, 0)


def lay_taps(wide, taps, rows):
    flat = wide.reshape(2, wide.shape[1] * 32, 128)

    def one(n):
        for b in range(3):
            shifted = flat[n, pl.ds(b, rows * 32), :].astype(BF16)
            taps[n, :, :, :, b * 128 : (b + 1) * 128] = shifted.reshape(rows // 2, 2, 32, 128)

    each_sample(one)


def pair_rows(taps, n, pairs):
    parts = [taps[n, q // 2 : q // 2 + pairs, q % 2].reshape(pairs * 32, WIDE) for q in range(4)]
    return jnp.concatenate(parts, axis=1)


def forward(taps, matrix, n, pairs):
    got = jnp.dot(pair_rows(taps, n, pairs), matrix[...], preferred_element_type=F32)
    return got.reshape(pairs, 32, 256)


def turned(left, right):
    return lax.dot_general(left, right, (((1,), (1,)), ((), ())), preferred_element_type=F32)


def backward(taps, matrix, n, pairs):
    return turned(pair_rows(taps, n, pairs), matrix[...]).reshape(pairs, 32, 256)


def lay_weights(weights, ahead, back):
    for q in range(4):
        for o in range(2):
            for b in range(3):
                tap, span = q - o, pl.ds(q * WIDE + b * 128, 128)
                inside = 0 <= tap <= 2
                lanes = pl.ds(o * 128, 128)
                ahead[span, lanes] = weights[tap * 3 + b] if inside else jnp.zeros((128, 128), BF16)
                back[lanes, span] = weights[(2 - tap) * 3 + 2 - b] if inside else jnp.zeros((128, 128), BF16)


def outer_sum(taps, grads, result, rows):
    total = None
    for n in range(2):
        part = lax.dot_general(
            taps[n].reshape(rows * 32, WIDE), grads[n].reshape(rows * 32, WIDE),
            (((0,), (0,)), ((), ())), preferred_element_type=F32,
        )
        total = part if total is None else total + part
    for a in range(3):
        for b in range(3):
            result[pl.ds((3 * a + b) * 128, 128)] = total[b * 128 : (b + 1) * 128, a * 128 : (a + 1) * 128]


def block_kernel(field, cotangent, w_one, w_two, output, field_grad, first_sum, second_sum, *scratch):
    (wide_f, wide_c, wide_h, wide_p, taps_f, taps_c, taps_h, taps_p, pre, grads_c, grads_p,
     ahead_one, back_one, ahead_two, back_two, first, second) = scratch[:17]
    halo_f = Halo(field, *scratch[17:22])
    halo_c = Halo(cotangent, *scratch[22:27])
    sum_two = Sum(second, second_sum, *scratch[27:31], scratch[31:36])
    sum_one = Sum(first, first_sum, *scratch[36:40], scratch[40:45])
    lat = lax.axis_index("lat")
    top = lat == 0
    at_pole = jnp.logical_or(top, lat == 7)

    barrier = pltpu.get_barrier_semaphore()

    def greet(device):
        pl.semaphore_signal(barrier, inc=1, device_id=device, device_id_type=pl.DeviceIdType.MESH)

    for v, h in SIDES:
        greet(halo_f.device(v, h))
    greet(sum_one.partner())
    sum_one.each(16, lambda step: greet(sum_one.plane_peer(step)[1]))
    sum_one.each(8, lambda step: greet(sum_one.column_peer(step)[1]))
    halo_f.pack()
    halo_c.pack()
    lay_weights(w_one, ahead_one, back_one)
    lay_weights(w_two, ahead_two, back_two)
    halo_f.fill(wide_f)
    halo_c.fill(wide_c)
    for wide in (wide_h, wide_p):
        wide[:, 34, :, :] = jnp.zeros((2, 32, 128), F32)
    grads_c[...] = jnp.zeros(grads_c.shape, BF16)
    grads_p[...] = jnp.zeros(grads_p.shape, BF16)
    for a in range(3):
        grads_c[:, a : a + 32, 0:24, a * 128 : (a + 1) * 128] = cotangent[...].reshape(2, 32, COLS, 128)

    pl.semaphore_wait(barrier, 31)
    halo_f.send()
    halo_c.send()
    halo_f.place(wide_f)
    lay_taps(wide_f, taps_f, 36)

    def pre_one(n):
        got = forward(taps_f, ahead_one, n, 17)
        for o in range(2):
            pre[n, pl.ds(o, 17, stride=2)] = got[:, :, o * 128 : (o + 1) * 128]

    each_sample(pre_one)

    @pl.when(at_pole)
    def _():
        row = jnp.where(top, 0, 33)
        for n in range(2):
            got = None
            for q in range(3):
                right = w_one[pl.ds(3 * (2 - q), 3)].reshape(WIDE, 128)
                part = jnp.dot(taps_f[n, (row + q) // 2, (row + q) % 2], right, preferred_element_type=F32)
                got = part if got is None else got + part
            pre[n, row] = got

    def hidden_one(n):
        value = pre[n]
        wide_h[n, 0:34] = value / (1.0 + jnp.exp(-value))

    each_sample(hidden_one)
    lay_taps(wide_h, taps_h, 34)
    outer_sum(taps_h, grads_c, second, 34)
    sum_two.start()

    halo_c.place(wide_c)
    lay_taps(wide_c, taps_c, 36)

    def hidden_grad_one(n):
        got = backward(taps_c, back_two, n, 17)
        for o in range(2):
            wide_p[n, pl.ds(o, 17, stride=2)] = got[:, :, o * 128 : (o + 1) * 128]

    each_sample(hidden_grad_one)
    sign = jnp.where(top, 1.0, -1.0)

    @pl.when(at_pole)
    def _():
        row = jnp.where(top, 0, 32)
        source = jnp.where(top, 0, 17)
        for n in range(2):
            left = taps_c[n, source].reshape(64, WIDE)
            change = turned(left, back_two[0:128, 768:1152]) - turned(left, back_two[0:128, 0:384])
            wide_p[n, pl.ds(row, 2)] += (sign * change).reshape(2, 32, 128)

    def pre_grad_one(n):
        value = pre[n]
        s = 1.0 / (1.0 + jnp.exp(-value))
        grad = wide_p[n, 0:34] * s * (1.0 + value * (1.0 - s))
        wide_p[n, 0:34] = grad
        place = lax.broadcasted_iota(jnp.int32, (32, 32, 128), 1)
        inner = jnp.where(jnp.logical_and(place >= 1, place <= 24), grad[1:33], 0.0).astype(BF16)
        for a in range(3):
            grads_p[n, pl.ds(1 + a, 32), :, a * 128 : (a + 1) * 128] = inner

    each_sample(pre_grad_one)
    sum_two.to_plane()
    outer_sum(taps_f, grads_p, first, 36)
    sum_one.start()
    sum_two.to_column()

    def output_one(n):
        got = forward(taps_h, ahead_two, n, 16)
        for o in range(2):
            kept = got[:, 0:24, o * 128 : (o + 1) * 128]
            output[n, :, o] = (field[n, :, o].astype(F32) + kept).astype(BF16)

    each_sample(output_one)
    sum_one.to_plane()
    sum_two.to_gather()
    lay_taps(wide_p, taps_p, 34)

    def field_grad_one(n):
        got = backward(taps_p, back_one, n, 16)
        for o in range(2):
            wide_f[n, pl.ds(o, 16, stride=2)] = got[:, :, o * 128 : (o + 1) * 128]

    each_sample(field_grad_one)

    @pl.when(at_pole)
    def _():
        row = jnp.where(top, 0, 31)
        source = jnp.where(top, 0, 33)
        for n in range(2):
            left = taps_p[n, source // 2, source % 2]
            change = turned(left, back_one[0:128, 768:1152]) - turned(left, back_one[0:128, 0:384])
            wide_f[n, row] += sign * change

    sum_one.to_column()

    def keep_one(n):
        kept = wide_f[n, 0:32, 0:24].reshape(PAIRS, 2, COLS, 128)
        field_grad[n] = (cotangent[n].astype(F32) + kept).astype(BF16)

    each_sample(keep_one)
    sum_two.to_share()
    sum_one.to_gather()
    sum_two.finish()
    sum_one.to_share()
    sum_one.finish()
    halo_f.close()
    halo_c.close()


def result_kernel(output, field_grad, first, second, output_out, field_grad_out, first_out, second_out, wide_one, wide_two, sems):
    copies = [
        pltpu.make_async_copy(output, output_out, sems.at[0]),
        pltpu.make_async_copy(field_grad, field_grad_out, sems.at[1]),
        pltpu.make_async_copy(wide_one, first_out, sems.at[2]),
        pltpu.make_async_copy(wide_two, second_out, sems.at[3]),
    ]
    copies[0].start()
    copies[1].start()
    for source, target, copy in ((first, wide_one, copies[2]), (second, wide_two, copies[3])):
        for half in range(2):
            for piece in range(16):
                row = half * HALF + ((9 * piece) // 2) * 8
                target[pl.ds(row, PIECE)] = source[half, piece].astype(F32)
        copy.start()
    for copy in copies:
        copy.wait()


def body(field, cotangent, first_weights, second_weights):
    vmem = pl.BlockSpec(memory_space=pltpu.VMEM)
    grad = jax.ShapeDtypeStruct((2, 16, PIECE, 128), BF16)
    whole = jax.ShapeDtypeStruct((2 * HALF, 128), F32)
    cells = jax.ShapeDtypeStruct((2, PAIRS, 2, COLS, 128), BF16)
    matrix = [pltpu.VMEM((4 * WIDE, 256), BF16), pltpu.VMEM((256, 4 * WIDE), BF16)]
    results = pl.pallas_call(
        block_kernel,
        out_shape=(cells, cells, grad, grad),
        in_specs=[vmem] * 4,
        out_specs=(vmem,) * 4,
        scratch_shapes=[
            pltpu.VMEM((2, 37, 32, 128), F32),
            pltpu.VMEM((2, 37, 32, 128), F32),
            pltpu.VMEM((2, 35, 32, 128), F32),
            pltpu.VMEM((2, 35, 32, 128), F32),
            pltpu.VMEM((2, 18, 2, 32, WIDE), BF16),
            pltpu.VMEM((2, 18, 2, 32, WIDE), BF16),
            pltpu.VMEM((2, 17, 2, 32, WIDE), BF16),
            pltpu.VMEM((2, 17, 2, 32, WIDE), BF16),
            pltpu.VMEM((2, 34, 32, 128), F32),
            pltpu.VMEM((2, 34, 32, WIDE), BF16),
            pltpu.VMEM((2, 36, 32, WIDE), BF16),
        ]
        + matrix
        + matrix
        + [pltpu.VMEM((2 * HALF, 128), F32)] * 2
        + halo_scratch()
        + halo_scratch()
        + sum_scratch()
        + sum_scratch(),
        compiler_params=pltpu.CompilerParams(
            collective_id=0, has_side_effects=True, vmem_limit_bytes=32 * 1024 * 1024
        ),
    )(field.reshape(cells.shape), cotangent.reshape(cells.shape), first_weights.reshape(9, 128, 128), second_weights.reshape(9, 128, 128))
    output, field_grad, first, second = pl.pallas_call(
        result_kernel,
        out_shape=(cells, cells, whole, whole),
        in_specs=[vmem] * 4,
        out_specs=(pl.BlockSpec(memory_space=pl.ANY),) * 4,
        scratch_shapes=[pltpu.VMEM((2 * HALF, 128), F32)] * 2 + [pltpu.SemaphoreType.DMA((4,))],
        compiler_params=pltpu.CompilerParams(vmem_limit_bytes=8 * 1024 * 1024),
    )(*results)
    first, second = first.reshape(3, 3, 128, 128), second.reshape(3, 3, 128, 128)
    return output.reshape(field.shape), field_grad.reshape(field.shape), first, second


def solution(mesh):
    return jax.shard_map(
        body,
        mesh=mesh,
        in_specs=(P(None, "lat", "lon", None), P(None, "lat", "lon", None), P(), P()),
        out_specs=(P(None, "lat", "lon", None), P(None, "lat", "lon", None), P(), P()),
        check_vma=False,
    )
```
